128 devices in a mesh: tok: 16 (over x_hi, z, core), wid: 8 (over y, x_lo).
Axes of the slice: x: 4 (x_hi: 2, x_lo: 2; x = x_hi * 2 + x_lo), y: 4, z: 4, core: 2. Of those that a mesh axis runs over, the one named last changes fastest.
Arguments:
- tokens: bfloat16 [9344, 1024], P('tok', 'wid'), may hold values from -6 to 6
- image_ids: int32 [9344], P('tok'), may hold values from 1 to 9360, as said below
- norm_gains: float32 [2, 2, 1024], P(None, None, 'wid'), may hold values from 0.5 to 1.5
- norm_shifts: float32 [2, 2, 1024], P(None, None, 'wid'), may hold values from -1.8 to 1.8
- qkv_weight: bfloat16 [2, 1024, 3, 1024], P(None, 'tok', None, 'wid'), may hold values from -0.1875 to 0.1875
- qv_bias: float32 [2, 2, 1024], P(None, None, 'wid'), may hold values from -3 to 3
- out_weight: bfloat16 [2, 1024, 1024], P(None, 'wid', 'tok'), may hold values from -0.75 to 0.75
- out_bias: float32 [2, 1024], P(None, 'wid'), may hold values from -3 to 3
- up_weight: bfloat16 [2, 1024, 4096], P(None, 'tok', 'wid'), may hold values from -0.1875 to 0.1875
- up_bias: float32 [2, 4096], P(None, 'wid'), may hold values from -3 to 3
- down_weight: bfloat16 [2, 4096, 1024], P(None, 'wid', 'tok'), may hold values from -0.125 to 0.125
- down_bias: float32 [2, 1024], P(None, 'wid'), may hold values from -3 to 3
- out_grad: bfloat16 [9344, 1024], P('tok', 'wid'), may hold values from -6 to 6
Outputs:
- activations: bfloat16 [9344, 1024], P('tok', 'wid')
- input_grad: float32 [9344, 1024], P('tok', 'wid')
- gain_grad: float32 [2, 2, 1024], P(None, None, 'wid')
- shift_grad: float32 [2, 2, 1024], P(None, None, 'wid')
- qkv_grad: float32 [2, 1024, 3, 1024], P(None, 'tok', None, 'wid')
- qv_bias_grad: float32 [2, 2, 1024], P(None, None, 'wid')
- out_weight_grad: float32 [2, 1024, 1024], P(None, 'wid', 'tok')
- out_bias_grad: float32 [2, 1024], P(None, 'wid')
- up_weight_grad: float32 [2, 1024, 4096], P(None, 'tok', 'wid')
- up_bias_grad: float32 [2, 4096], P(None, 'wid')
- down_weight_grad: float32 [2, 4096, 1024], P(None, 'wid', 'tok')
- down_bias_grad: float32 [2, 1024], P(None, 'wid')
The draws below stay inside these ranges and needn't reach their ends.
Inputs may be any that keep to these rules, and one draw needn't show every extreme that they name: `image_ids`: images 1 to 16, in order, each hold exactly 577 consecutive tokens; each aligned block of 584 tokens holds one whole image; every other token has a number of its own above 16, and the last token of each block is such a token.
All inputs are finite; a program needn't handle non-finite values.
Results may differ from the reference program's by a relative error of at most 0.02.
Values may be sent and summed in bfloat16 or wider, within the bound.
No kernel may reach another device: no remote copies, remote signals or barrier semaphores. Data moves between devices by JAX's collectives and lax.ppermute only.
A program may use at most 128 MiB of HBM per device.

```python
import jax
import jax.numpy as jnp
from jax import lax

D = 1024
HEADS = 16
HEAD = 64
FF = 4096
LENGTH = 577
LAYERS = 2
IMG_DEV = 1
TOK_DEV = 584
TOKENS = 9344
IMAGES = 16
N_TOK = 16


def draw_image_ids(key, part):
    blocks = TOKENS // TOK_DEV
    spare = TOK_DEV - IMG_DEV * LENGTH
    offsets = jax.random.randint(key, (blocks,), 0, spare).astype(jnp.int32)
    position = jnp.arange(TOKENS, dtype=jnp.int32)
    block = position // TOK_DEV
    local = position - block * TOK_DEV - offsets[block]
    inside = (local >= 0) & (local < IMG_DEV * LENGTH)
    number = block * IMG_DEV + jnp.maximum(local, 0) // LENGTH + 1
    return jnp.where(inside, number, IMAGES + 1 + position).astype(jnp.int32)


def level_of(key, dims, split, low, largest):
    level, own = 1.0, jax.random.fold_in(key, 6)
    for dim, parts in split:
        steps = jnp.exp(jax.random.uniform(jax.random.fold_in(own, dim), (parts,), jnp.float32, low / len(split), largest / len(split)))
        level = level * jnp.repeat(steps, dims[dim] // parts).reshape([-1 if axis == dim else 1 for axis in range(len(dims))])
    return level


def normal_values(rng, shape, scale, reach, split=(), held_as=jnp.bfloat16):
    loudness = level_of(rng, shape, split, -0.22, 0.18) if split else 1.0
    drawn = jax.random.normal(rng, shape, jnp.float32) * scale * loudness
    return jnp.minimum(jnp.maximum(drawn, -reach), reach).astype(held_as)


def setup_inputs(seed: int = 0) -> dict:
    seeds = jax.random.split(jax.random.key(seed), 14)
    return {
        "tokens": normal_values(seeds[0], (TOKENS, D), 1.0, 6.0, ((0, 16), (1, 8))),
        "image_ids": draw_image_ids(jax.random.fold_in(seeds[13], 71), 0),
        "norm_gains": jnp.clip(1.0 + 0.1 * jax.random.normal(seeds[2], (LAYERS, 2, D), jnp.float32), 0.5, 1.5),
        "norm_shifts": normal_values(seeds[3], (LAYERS, 2, D), 0.3, 1.8, ((2, 8),), jnp.float32),
        "qkv_weight": normal_values(seeds[4], (LAYERS, D, 3, D), D ** -0.5, 0.1875, ((1, 16), (3, 8))),
        "qv_bias": normal_values(seeds[5], (LAYERS, 2, D), 0.5, 3.0, ((2, 8),), jnp.float32),
        "out_weight": normal_values(seeds[6], (LAYERS, D, D), (D // 16) ** -0.5, 0.75, ((1, 8), (2, 16))),
        "out_bias": normal_values(seeds[7], (LAYERS, D), 0.5, 3.0, ((1, 8),), jnp.float32),
        "up_weight": normal_values(seeds[8], (LAYERS, D, FF), D ** -0.5, 0.1875, ((1, 16), (2, 8))),
        "up_bias": normal_values(seeds[9], (LAYERS, FF), 0.5, 3.0, ((1, 8),), jnp.float32),
        "down_weight": normal_values(seeds[10], (LAYERS, FF, D), (FF // 2) ** -0.5, 0.125, ((1, 8), (2, 16))),
        "down_bias": normal_values(seeds[11], (LAYERS, D), 0.5, 3.0, ((1, 8),), jnp.float32),
        "out_grad": normal_values(seeds[12], (TOKENS, D), 1.0, 6.0, ((0, 16), (1, 8))),
    }


EPSILON = 1e-06
HIGH = lax.Precision.HIGHEST

@jax.custom_vjp
def low(v):
    return lax.optimization_barrier(v.astype(jnp.bfloat16)).astype(jnp.float32)

@jax.custom_vjp
def low_back(v):
    return v

def low_keep(v):
    return (low(v), None)

def low_pass(kept, grad):
    return (grad,)

def back_keep(v):
    return (v, None)

def back_low(kept, grad):
    return (low(grad),)
low.defvjp(low_keep, low_pass)
low_back.defvjp(back_keep, back_low)

def layer_norm(values, gain, shift):
    mean = lax.optimization_barrier(jnp.mean(values, axis=-1, keepdims=True))
    spread = lax.optimization_barrier(jnp.mean(jnp.square(values - mean), axis=-1, keepdims=True))
    return (values - mean) * lax.rsqrt(spread + EPSILON) * gain + shift

def attention(query, keys, values, image_ids):

    @jax.checkpoint
    def block(start):
        query_blk = lax.dynamic_slice_in_dim(query, start, TOK_DEV, 0).reshape(TOK_DEV, HEADS, HEAD)
        key_blk = lax.dynamic_slice_in_dim(keys, start, TOK_DEV, 0).reshape(TOK_DEV, HEADS, HEAD)
        value_blk = lax.dynamic_slice_in_dim(values, start, TOK_DEV, 0).reshape(TOK_DEV, HEADS, HEAD)
        block_ids = lax.dynamic_slice_in_dim(image_ids, start, TOK_DEV, 0)
        scores = jnp.einsum('qhe,khe->hqk', query_blk, key_blk, precision=HIGH) * HEAD ** (-0.5)
        scores = low_back(scores)
        allowed = block_ids[:, None] == block_ids[None, :]
        scores = jnp.where(allowed[None], scores, -1e+30)
        top = lax.optimization_barrier(jnp.max(scores, axis=2, keepdims=True))
        expo = jnp.exp(scores - top)
        total = lax.optimization_barrier(jnp.sum(expo, axis=2, keepdims=True))
        probs = low(expo / total)
        mixed = jnp.einsum('hqk,khe->qhe', probs, value_blk, precision=HIGH)
        return mixed.reshape(TOK_DEV, D)
    starts = jnp.arange(N_TOK, dtype=jnp.int32) * TOK_DEV
    return lax.map(block, starts).reshape(TOKENS, D)

def forward(state, params, image_ids):
    gains, shifts, qkv, qv_b, w_out, b_out, w_up, b_up, w_down, b_down = params
    for layer in range(LAYERS):
        normed = low(layer_norm(state, gains[layer, 0], shifts[layer, 0]))
        proj = jnp.einsum('td,dcf->tcf', normed, qkv[layer], precision=HIGH)
        query = low_back(low(proj[:, 0] + qv_b[layer, 0]))
        keys = low_back(low(proj[:, 1]))
        values = low_back(low(proj[:, 2] + qv_b[layer, 1]))
        attended = low_back(low(attention(query, keys, values, image_ids)))
        state = state + low_back(jnp.dot(attended, w_out[layer], precision=HIGH) + b_out[layer])
        normed = low(layer_norm(state, gains[layer, 1], shifts[layer, 1]))
        pre = low_back(jnp.dot(normed, w_up[layer], precision=HIGH) + b_up[layer])
        hidden = low(jax.nn.gelu(pre, approximate=False))
        state = state + low_back(jnp.dot(hidden, w_down[layer], precision=HIGH) + b_down[layer])
    return state

def reference(tokens, image_ids, norm_gains, norm_shifts, qkv_weight, qv_bias, out_weight, out_bias, up_weight, up_bias, down_weight, down_bias, out_grad):
    params = (norm_gains.astype(jnp.float32), norm_shifts.astype(jnp.float32), qkv_weight.astype(jnp.float32), qv_bias.astype(jnp.float32), out_weight.astype(jnp.float32), out_bias.astype(jnp.float32), up_weight.astype(jnp.float32), up_bias.astype(jnp.float32), down_weight.astype(jnp.float32), down_bias.astype(jnp.float32))
    start = tokens.astype(jnp.float32)
    result, pullback = jax.vjp(lambda values, weights: forward(values, weights, image_ids), start, params)
    grad_input, grads = pullback(out_grad.astype(jnp.float32))
    return (result.astype(jnp.bfloat16), grad_input, grads[0], grads[1], grads[2], grads[3], grads[4], grads[5], grads[6], grads[7], grads[8], grads[9])
```

```python
import functools

import jax
import jax.numpy as jnp
from jax import lax
from jax.experimental import pallas as pl
from jax.experimental.pallas import tpu as pltpu
from jax.sharding import PartitionSpec as P

HEAD = 64
LAYERS = 2
EPSILON = 1e-06
LANES = 128
BF16 = jnp.bfloat16
F32 = jnp.float32
VMEM_LIMIT = 20 * 1024 * 1024


def swap(value, axis, mask):
    pairs = [(i, i ^ mask) for i in range(lax.axis_size(axis))]
    return lax.ppermute(value, axis, pairs)


def gather_blocks(block):
    b1 = swap(block, "wid", 1)
    b2 = swap(block, "wid", 2)
    b6 = swap(block, "wid", 6)
    b4 = swap(block, "wid", 4)
    b3 = swap(b1, "wid", 2)
    b7 = swap(b1, "wid", 6)
    b5 = swap(b4, "wid", 1)
    return (block, b1, b2, b3, b4, b5, b6, b7)


def copies_to_all(value, axis):
    copies = jnp.broadcast_to(value, (lax.axis_size(axis), *value.shape))
    return lax.all_to_all(copies, axis, split_axis=0, concat_axis=0, tiled=True)


def add_up(*terms):
    return functools.reduce(jnp.add, [t.astype(F32) for t in terms])


def reduce_blocks(parts):
    for_pair = [swap(parts[3], "wid", 2), swap(parts[7], "wid", 6)]
    for_far = swap(parts[5], "wid", 1)
    near = [swap(parts[2], "wid", 2), swap(parts[6], "wid", 6)]
    far = swap(add_up(parts[4], for_far).astype(BF16), "wid", 4)
    pair = swap(add_up(parts[1], *for_pair).astype(BF16), "wid", 1)
    return add_up(parts[0], *near, far, pair)


def scatter_sum(parts):
    other = swap(parts[1], "tok", 1)
    sums = [add_up(parts[0, z], other[z]).astype(BF16) for z in range(4)]
    line = [swap(sums[z], "tok", 2 * z) for z in (2, 1, 3)]
    both = [add_up(sums[0][h], *[p[h] for p in line]) for h in range(2)]
    return both[0] + swap(both[1].astype(BF16), "tok", 8).astype(F32)


def dot_nn(a, b):
    return lax.dot_general(a, b, (((1,), (0,)), ((), ())), preferred_element_type=F32)


def dot_nt(a, b):
    return lax.dot_general(a, b, (((1,), (1,)), ((), ())), preferred_element_type=F32)


def dot_tn(a, b):
    return lax.dot_general(a, b, (((0,), (0,)), ((), ())), preferred_element_type=F32)


def over_rows(rows, size, body):
    count = rows // size

    def step(i, carry):
        body(pl.multiple_of(i * size, size), size)
        return carry

    lax.fori_loop(0, count, step, 0)
    if rows % size:
        body(count * size, rows % size)


def row_chunks(rows, count):
    step = rows // count // 16 * 16
    starts = [i * step for i in range(count)]
    return [(s, step if i + 1 < count else rows - s) for i, s in enumerate(starts)]


def place(me, slot):
    return pl.ds(pl.multiple_of((me ^ slot) * LANES, LANES), LANES)


def norm_rows(me, blocks, base, gains, shifts, x_ref, n_ref, xh_ref, r_ref):
    rows = n_ref.shape[0]
    count = len(blocks)
    width = count * LANES

    def body(start, size):
        at = pl.ds(start, size)
        vals = []
        for k, ref in enumerate(blocks):
            v = ref[at, :].astype(F32)
            if base is not None:
                v = v + base[at, place(me, k)]
            x_ref[at, place(me, k)] = v
            vals.append(v)
        mean = jnp.sum(functools.reduce(jnp.add, vals), axis=1, keepdims=True) / width
        vals = [v - mean for v in vals]
        spread = functools.reduce(jnp.add, [v * v for v in vals])
        spread = jnp.sum(spread, axis=1, keepdims=True) / width
        scale = lax.rsqrt(spread + EPSILON)
        r_ref[at, :] = jnp.broadcast_to(scale, (size, LANES))
        for k, v in enumerate(vals):
            xh = v * scale
            xh_ref[at, place(me, k)] = xh.astype(BF16)
            n_ref[at, place(me, k)] = (xh * gains(me ^ k) + shifts(me ^ k)).astype(BF16)

    over_rows(rows, 32, body)


def norm_back_rows(me, blocks, base, xh_ref, r_ref, g_ref, low_ref):
    rows = low_ref.shape[0]
    width = len(blocks) * LANES

    def body(start, size):
        at = pl.ds(start, size)
        vals = [ref[at, :].astype(F32) for ref in blocks]
        xhs = [xh_ref[at, place(me, k)].astype(F32) for k in range(len(blocks))]
        one = jnp.sum(functools.reduce(jnp.add, vals), axis=1, keepdims=True) / width
        two = functools.reduce(jnp.add, [v * x for v, x in zip(vals, xhs)])
        two = jnp.sum(two, axis=1, keepdims=True) / width
        scale = r_ref[at, :]
        for k, (v, x) in enumerate(zip(vals, xhs)):
            g = base[at, place(me, k)] + scale * (v - one - x * two)
            g_ref[at, place(me, k)] = g
            low_ref[at, place(me, k)] = g.astype(BF16)

    over_rows(rows, 32, body)


def partial_blocks(me, left, weight_ref, cols, part_refs):
    odd = lax.rem(me, 2) == 1
    for k in range(0, len(part_refs), 2):
        start = pl.multiple_of(((me // 2) ^ (k // 2)) * 2 * LANES, 2 * LANES)
        both = dot_nt(left, weight_ref[pl.ds(start, 2 * LANES), cols]).astype(BF16)
        low, high = both[:, :LANES], both[:, LANES:]
        part_refs[k][...] = jnp.where(odd, high, low)
        part_refs[k + 1][...] = jnp.where(odd, low, high)


def head_masks():
    lane = lax.broadcasted_iota(jnp.int32, (1, LANES), 1)
    return [(lane >= h * HEAD) & (lane < (h + 1) * HEAD) for h in range(LANES // HEAD)]


def head_scores(query, keys, allowed):
    return jnp.where(allowed, dot_nt(query, keys) * HEAD ** (-0.5), -1e30)


def erf_of(x):
    return lax.erf(x)


def attend_kernel(first, row, *refs):
    refs = list(refs)
    me_ref = refs[0]
    if first:
        par_ref = refs.pop()
        blocks, base, refs = refs[1:9], None, refs[9:]
        rows = blocks[0].shape[0] - 2 * par_ref.shape[1]
        for k, ref in enumerate(blocks):
            tail = ref[rows:, :].astype(F32)
            par_ref[me_ref[0] ^ k] = tail[: par_ref.shape[1]] + tail[par_ref.shape[1] :]
    else:
        par_ref, blocks, base, refs = refs[1], refs[2:10], refs[10], refs[11:]
    idr_ref, idc_ref, w_ref, qvb_ref = refs[:4]
    x_ref, n_ref, xh_ref, r_ref, qkv_ref, lse_ref, o_ref = refs[4:11]
    part_refs = refs[11:19]
    me = me_ref[0]
    rows = n_ref.shape[0]
    norm_rows(
        me,
        blocks,
        base,
        lambda j: par_ref[j, row : row + 1, :],
        lambda j: par_ref[j, row + 4 : row + 5, :],
        x_ref,
        n_ref,
        xh_ref,
        r_ref,
    )
    qkv = dot_nn(n_ref[...], w_ref[:, : 3 * LANES])
    qkv_ref[:, :LANES] = (qkv[:, :LANES] + qvb_ref[0:1, :]).astype(BF16)
    qkv_ref[:, LANES : 2 * LANES] = qkv[:, LANES : 2 * LANES].astype(BF16)
    qkv_ref[:, 2 * LANES :] = (qkv[:, 2 * LANES :] + qvb_ref[1:2, :]).astype(BF16)
    keys = qkv_ref[:, LANES : 2 * LANES]
    values = qkv_ref[:, 2 * LANES :]
    masks = head_masks()
    for start, size in row_chunks(rows, 4):
        query = qkv_ref[start : start + size, :LANES]
        allowed = idc_ref[start : start + size, :1] == idr_ref[...]
        mixed = jnp.zeros((size, LANES), F32)
        logsum = jnp.zeros((size, LANES), F32)
        for mask in masks:
            own = jnp.where(mask, query, jnp.zeros_like(query))
            scores = head_scores(own, keys, allowed)
            top = jnp.max(scores, axis=1, keepdims=True)
            expo = jnp.exp(scores - top)
            total = jnp.sum(expo, axis=1, keepdims=True)
            probs = (expo * (1.0 / total)).astype(BF16)
            mixed = jnp.where(mask, dot_nn(probs, values), mixed)
            logsum = jnp.where(mask, top + jnp.log(total), logsum)
        lse_ref[start : start + size, :] = logsum
        o_ref[start : start + size, :] = mixed.astype(BF16)
    partial_blocks(me, o_ref[...], w_ref, slice(3 * LANES, 4 * LANES), part_refs)


def feed_kernel(row, *refs):
    me_ref, par_ref = refs[:2]
    blocks = refs[2:10]
    base, w_ref, b_ref = refs[10:13]
    x_ref, n_ref, xh_ref, r_ref, h_ref, slope_ref = refs[13:19]
    part_refs, u_ref = refs[19:27], refs[27]
    me = me_ref[0]
    rows = n_ref.shape[0]
    ff = h_ref.shape[1]
    norm_rows(
        me,
        blocks,
        base,
        lambda j: par_ref[j, row : row + 1, :],
        lambda j: par_ref[j, row + 4 : row + 5, :],
        x_ref,
        n_ref,
        xh_ref,
        r_ref,
    )
    u_ref[...] = dot_nn(n_ref[...], w_ref[:, :ff])

    def body(start, size):
        at = pl.ds(start, size)
        u = u_ref[at, :] + b_ref[...]
        phi = 0.5 * (1.0 + erf_of(u * 0.7071067811865476))
        h_ref[at, :] = (u * phi).astype(BF16)
        slope_ref[at, :] = phi + u * jnp.exp(-0.5 * u * u) * 0.3989422804014327

    over_rows(rows, 32, body)
    partial_blocks(me, h_ref[...], w_ref, slice(ff, 2 * ff), part_refs)


def feed_back_kernel(first, *refs):
    refs = list(refs)
    me_ref = refs[0]
    blocks = refs[1:9]
    if first:
        w_ref, slope_ref, g_ref, low_ref, du_ref = refs[9:14]
    else:
        base, xh_ref, r_ref, w_ref, slope_ref, g_ref, low_ref, du_ref = refs[9:17]
    part_refs, dh_ref = refs[-9:-1], refs[-1]
    me = me_ref[0]
    rows, ff = slope_ref.shape
    if first:

        def copy(start, size):
            at = pl.ds(start, size)
            for k, ref in enumerate(blocks):
                low_ref[at, place(me, k)] = ref[at, :]
                g_ref[at, place(me, k)] = ref[at, :].astype(F32)

        over_rows(rows, 32, copy)
    else:
        norm_back_rows(me, blocks, base, xh_ref, r_ref, g_ref, low_ref)
    dh_ref[...] = dot_nn(low_ref[...], w_ref[:, ff:])

    def body(start, size):
        at = pl.ds(start, size)
        du_ref[at, :] = (dh_ref[at, :] * slope_ref[at, :]).astype(BF16)

    over_rows(rows, 32, body)
    partial_blocks(me, du_ref[...], w_ref, slice(0, ff), part_refs)


def attend_back_kernel(*refs):
    me_ref = refs[0]
    blocks = refs[1:9]
    base, xh_ref, r_ref, w_ref, qkv_ref, lse_ref, idr_ref, idc_ref = refs[9:17]
    g_ref, low_ref, dproj_ref = refs[17:20]
    part_refs = refs[20:28]
    do_ref, p_ref, ds_ref = refs[28:]
    me = me_ref[0]
    rows = low_ref.shape[0]
    norm_back_rows(me, blocks, base, xh_ref, r_ref, g_ref, low_ref)
    do_ref[...] = dot_nn(low_ref[...], w_ref[:, 3 * LANES :]).astype(BF16)
    keys = qkv_ref[:, LANES : 2 * LANES]
    values = qkv_ref[:, 2 * LANES :]
    scale = HEAD ** (-0.5)
    dk = jnp.zeros((rows, LANES), F32)
    dv = jnp.zeros((rows, LANES), F32)
    masks = head_masks()
    for h, mask in enumerate(masks):
        for start, size in row_chunks(rows, 4):
            end = start + size
            query = qkv_ref[start:end, :LANES]
            own = jnp.where(mask, query, jnp.zeros_like(query))
            allowed = idc_ref[start:end, :1] == idr_ref[...]
            scores = head_scores(own, keys, allowed)
            probs = jnp.exp(scores - lse_ref[start:end, h * HEAD : h * HEAD + 1])
            p_ref[start:end, :] = probs.astype(BF16)
            dmix = do_ref[start:end, :]
            dmix = jnp.where(mask, dmix, jnp.zeros_like(dmix))
            dprobs = dot_nt(dmix, values)
            centre = jnp.sum(probs * dprobs, axis=1, keepdims=True)
            ds = (probs * (dprobs - centre)).astype(BF16)
            ds_ref[start:end, :] = ds
            dq = (dot_nn(ds, keys) * scale).astype(BF16)
            if h == 0:
                dproj_ref[start:end, :LANES] = dq
            else:
                dproj_ref[start:end, :LANES] = jnp.where(mask, dq, dproj_ref[start:end, :LANES])
        dv = jnp.where(mask, dot_tn(p_ref[...], do_ref[...]), dv)
        dk = jnp.where(mask, dot_tn(ds_ref[...], qkv_ref[:, :LANES]), dk)
    dproj_ref[:, LANES : 2 * LANES] = (dk * scale).astype(BF16)
    dproj_ref[:, 2 * LANES :] = dv.astype(BF16)
    partial_blocks(me, dproj_ref[...], w_ref, slice(0, 3 * LANES), part_refs)


def weight_grad_kernel(me_ref, xa_ref, ya_ref, xb_ref, yb_ref, out_ref):
    split = ya_ref.shape[1]
    step = 256
    shard = xa_ref.shape[1] // 16
    me = me_ref[0]
    for i in range(0, xa_ref.shape[1], step):
        da = dot_tn(xa_ref[:, i : i + step], ya_ref[...]).astype(BF16)
        db = dot_tn(xb_ref[:, i : i + step], yb_ref[...]).astype(BF16)
        if len(out_ref.shape) == 2:
            out_ref[i : i + step, :split] = da
            out_ref[i : i + step, split:] = db
        else:
            for s in range(0, step, shard):
                to = me ^ ((i + s) // shard)
                c, z, h = to & 1, (to >> 1) & 3, to >> 3
                out_ref[c, z, h, :, :split] = da[s : s + shard]
                out_ref[c, z, h, :, split:] = db[s : s + shard]


def whole(kernel, outs, scratch, name, flops, *args):
    vmem = pl.BlockSpec(memory_space=pltpu.VMEM)
    smem = pl.BlockSpec(memory_space=pltpu.SMEM)
    size = sum(a.size * a.dtype.itemsize for a in args)
    size += sum(o.size * o.dtype.itemsize for o in outs)
    return pl.pallas_call(
        kernel,
        out_shape=outs,
        in_specs=[smem if a.shape == (1,) else vmem for a in args],
        out_specs=[vmem] * len(outs),
        scratch_shapes=scratch,
        compiler_params=pltpu.CompilerParams(vmem_limit_bytes=VMEM_LIMIT),
        cost_estimate=pl.CostEstimate(flops=flops, bytes_accessed=size, transcendentals=0),
        name=name,
    )(*args)


def shards(
    tokens,
    image_ids,
    norm_gains,
    norm_shifts,
    qkv_weight,
    qv_bias,
    out_weight,
    out_bias,
    up_weight,
    up_bias,
    down_weight,
    down_bias,
    out_grad,
):
    rows, cols = tokens.shape
    peers = lax.axis_size("wid")
    width = cols * peers
    ff = up_weight.shape[2]
    me = lax.axis_index("wid")
    me1 = me.astype(jnp.int32).reshape(1)

    def arr(shape, dtype):
        return jax.ShapeDtypeStruct(shape, dtype)

    full32 = arr((rows, width), F32)
    full16 = arr((rows, width), BF16)
    own32 = arr((rows, cols), F32)
    own16 = arr((rows, cols), BF16)
    parts16 = [own16] * peers
    met = lax.axis_index("tok").astype(jnp.int32).reshape(1)
    shard = width // lax.axis_size("tok")

    down_t = jnp.swapaxes(down_weight, 1, 2)
    out_t = jnp.swapaxes(out_weight, 1, 2)
    mix_local = [
        jnp.concatenate([qkv_weight[l].reshape(-1, 3 * cols), out_t[l]], axis=1)
        for l in range(LAYERS)
    ]
    feed_local = [jnp.concatenate([up_weight[l], down_t[l]], axis=1) for l in range(LAYERS)]

    small = jnp.concatenate([norm_gains.reshape(-1, cols), norm_shifts.reshape(-1, cols)])
    high = lax.reduce_precision(small, 8, 7)
    rest = lax.reduce_precision(small - high, 8, 7)
    blocks = gather_blocks(
        jnp.concatenate([tokens, high.astype(BF16), rest.astype(BF16)], axis=0)
    )
    mix_w = [copies_to_all(mix_local[0], "tok").reshape(width, 4 * cols)]
    pars = None
    feed_w = [lax.all_gather(feed_local[0], "tok", axis=0, tiled=True)]
    mix_w.append(lax.all_gather(mix_local[1], "tok", axis=0, tiled=True))
    feed_w.append(lax.all_gather(feed_local[1], "tok", axis=0, tiled=True))

    idr = image_ids.reshape(1, rows)
    idc = jnp.broadcast_to(image_ids[:, None], (rows, LANES))

    mm = 2 * rows * width
    base = None
    saved = []
    for l in range(LAYERS):
        first = base is None
        x, n1, xh1, r1, qkv, lse, o, *part = whole(
            functools.partial(attend_kernel, first, 2 * l),
            [full32, full16, full16, own32, arr((rows, 3 * cols), BF16), own32, own16, *parts16]
            + [arr((peers, *small.shape), F32)] * first,
            [],
            "attend",
            mm * 4 * cols + 8 * rows * rows * cols,
            me1,
            *(() if first else (pars,)),
            *blocks,
            *(() if first else (base,)),
            idr,
            idc,
            mix_w[l],
            qv_bias[l],
        )
        if first:
            pars = part.pop()
        blocks = gather_blocks((reduce_blocks(part) + out_bias[l]).astype(BF16))
        mid, n2, xh2, r2, h, slope, *part = whole(
            functools.partial(feed_kernel, 2 * l + 1),
            [
                full32,
                full16,
                full16,
                own32,
                arr((rows, ff), BF16),
                arr((rows, ff), F32),
                *parts16,
            ],
            [pltpu.VMEM((rows, ff), F32)],
            "feed",
            mm * 2 * ff,
            me1,
            pars,
            *blocks,
            x,
            feed_w[l],
            up_bias[l].reshape(1, ff),
        )
        branch = reduce_blocks(part) + down_bias[l]
        base = mid
        if l + 1 < LAYERS:
            blocks = gather_blocks(branch.astype(BF16))
        saved.append((n1, xh1, r1, qkv, lse, o, n2, xh2, r2, h, slope))
    state = lax.dynamic_slice_in_dim(base, me * cols, cols, 1) + branch
    activations = state.astype(BF16)

    blocks = gather_blocks(out_grad)
    g = None
    results = []
    for l in reversed(range(LAYERS)):
        n1, xh1, r1, qkv, lse, o, n2, xh2, r2, h, slope = saved[l]
        extra = () if g is None else (g, xh_up, r_up)
        g, gm, du, *part = whole(
            functools.partial(feed_back_kernel, g is None),
            [full32, full16, arr((rows, ff), BF16), *parts16],
            [pltpu.VMEM((rows, ff), F32)],
            "feed_back",
            mm * 2 * ff,
            me1,
            *blocks,
            *extra,
            feed_w[l],
            slope,
        )
        dn2 = reduce_blocks(part)
        blocks = gather_blocks((dn2 * norm_gains[l, 1]).astype(BF16))
        (dfeed,) = whole(
            weight_grad_kernel,
            [arr((width, 2 * ff) if l else (2, 4, 2, shard, 2 * ff), BF16)],
            [],
            "feed_grad",
            mm * 2 * ff,
            met,
            n2,
            du,
            gm,
            h,
        )
        g, ga, dproj, *part = whole(
            attend_back_kernel,
            [full32, full16, arr((rows, 3 * cols), BF16), *parts16],
            [
                pltpu.VMEM((rows, cols), BF16),
                pltpu.VMEM((rows, rows), BF16),
                pltpu.VMEM((rows, rows), BF16),
            ],
            "attend_back",
            mm * 4 * cols + 20 * rows * rows * cols,
            me1,
            *blocks,
            g,
            xh2,
            r2,
            mix_w[l],
            qkv,
            lse,
            idr,
            idc,
        )
        dn1 = reduce_blocks(part)
        (dmix,) = whole(
            weight_grad_kernel,
            [arr((width, 4 * cols) if l else (2, 4, 2, shard, 4 * cols), BF16)],
            [],
            "attend_grad",
            mm * 4 * cols,
            met,
            n1,
            dproj,
            ga,
            o,
        )
        own = lambda a: lax.dynamic_slice_in_dim(a, me * cols, cols, 1).astype(F32)
        xo1 = own(xh1)
        a1 = dn1 * norm_gains[l, 0]
        if l:
            blocks = gather_blocks(a1.astype(BF16))
            xh_up, r_up = xh1, r1
        else:
            sums = jnp.concatenate([jnp.sum(a1, axis=1), jnp.sum(a1 * xo1, axis=1)])
            sums = copies_to_all(sums.reshape(1, -1), "wid").sum(axis=0).reshape(-1)
            one, two = sums[:rows, None] / width, sums[rows:, None] / width
            input_grad = own(g) + r1 * (a1 - one - xo1 * two)
        vectors = [
            jnp.sum(dn1 * xo1, axis=0),
            jnp.sum(dn2 * own(xh2), axis=0),
            jnp.sum(dn1, axis=0),
            jnp.sum(dn2, axis=0),
            jnp.sum(dproj[:, :cols].astype(F32), axis=0),
            jnp.sum(dproj[:, 2 * cols :].astype(F32), axis=0),
            jnp.sum(own(ga), axis=0),
            jnp.sum(own(gm), axis=0),
            jnp.sum(du.astype(F32), axis=0),
        ]
        if l:
            scattered = [
                lax.psum_scatter(a, "tok", scatter_dimension=0, tiled=True).astype(F32)
                for a in (dfeed, dmix)
            ]
        else:
            scattered = [scatter_sum(dfeed), scatter_sum(dmix)]
        results.append((jnp.concatenate(vectors).reshape(-1, cols), scattered))
    results = results[::-1]
    lines = jnp.stack([line for line, _ in results])
    lines = copies_to_all(lines, "tok").reshape(-1, *lines.shape).sum(axis=0)
    results = [(lines[l], results[l][1]) for l in range(LAYERS)]

    def stack(pick):
        return jnp.stack([pick(line, big) for line, big in results])

    return (
        activations,
        input_grad,
        stack(lambda v, b: v[0:2]),
        stack(lambda v, b: v[2:4]),
        stack(lambda v, b: b[1][:, : 3 * cols].reshape(-1, 3, cols)),
        stack(lambda v, b: v[4:6]),
        jnp.swapaxes(stack(lambda v, b: b[1][:, 3 * cols :]), 1, 2),
        stack(lambda v, b: v[6]),
        stack(lambda v, b: b[0][:, :ff]),
        stack(lambda v, b: v[8:].reshape(-1)),
        jnp.swapaxes(stack(lambda v, b: b[0][:, ff:]), 1, 2),
        stack(lambda v, b: v[7]),
    )


def solution(mesh):
    placed = (
        P("tok", "wid"),
        P("tok"),
        P(None, None, "wid"),
        P(None, None, "wid"),
        P(None, "tok", None, "wid"),
        P(None, None, "wid"),
        P(None, "wid", "tok"),
        P(None, "wid"),
        P(None, "tok", "wid"),
        P(None, "wid"),
        P(None, "wid", "tok"),
        P(None, "wid"),
        P("tok", "wid"),
    )
    return jax.shard_map(
        shards,
        mesh=mesh,
        in_specs=placed,
        out_specs=(
            P("tok", "wid"),
            P("tok", "wid"),
            P(None, None, "wid"),
            P(None, None, "wid"),
            P(None, "tok", None, "wid"),
            P(None, None, "wid"),
            P(None, "wid", "tok"),
            P(None, "wid"),
            P(None, "tok", "wid"),
            P(None, "wid"),
            P(None, "wid", "tok"),
            P(None, "wid"),
        ),
        check_vma=False,
    )
```

```python
import functools
import types

import jax
import jax.numpy as jnp
from jax import lax
from jax.experimental import pallas as pl
from jax.experimental.pallas import tpu as pltpu
from jax.sharding import PartitionSpec as P

HEAD = 64
LAYERS = 2
EPSILON = 1e-06
LANES = 128
BF16 = jnp.bfloat16
F32 = jnp.float32
VMEM_LIMIT = 30 * 1024 * 1024


def swap(value, axis, mask):
    pairs = [(i, i ^ mask) for i in range(lax.axis_size(axis))]
    return lax.ppermute(value, axis, pairs)


def gather_blocks(block):
    b4 = swap(block, "wid", 4)
    b1 = swap(block, "wid", 1)
    b2 = swap(block, "wid", 2)
    b6 = swap(block, "wid", 6)
    b3 = swap(b1, "wid", 2)
    b7 = swap(b1, "wid", 6)
    b5 = swap(b4, "wid", 1)
    return (block, b1, b2, b3, b4, b5, b6, b7)


def copies_to_all(value, axis):
    copies = jnp.broadcast_to(value, (lax.axis_size(axis), *value.shape))
    return lax.all_to_all(copies, axis, split_axis=0, concat_axis=0, tiled=True)


def add_up(*terms):
    return functools.reduce(jnp.add, [t.astype(F32) for t in terms])


def reduce_blocks(parts):
    p0, p1, p23, p4, p5, p67 = parts
    s5 = swap(p5, "wid", 1)
    s23 = swap(p23, "wid", 2)
    s67 = swap(p67, "wid", 6)
    far = swap(add_up(p4, s5).astype(BF16), "wid", 4)
    pair = swap(add_up(p1, s23[1], s67[1]).astype(BF16), "wid", 1)
    return add_up(p0, s23[0], s67[0], far, pair), s23


def gather_planes(block, early, late):
    far = after(swap(block, "tok", 8), *early)
    pair = jnp.stack([block, far])
    third = after(swap(pair, "tok", 6), *late)
    own = jnp.stack([pair, swap(pair, "tok", 2), swap(pair, "tok", 4), third])
    return own, swap(own, "tok", 1)


def scatter_pairs(parts):
    other = swap(parts[1], "tok", 1)
    return [add_up(parts[0, z], other[z]).astype(BF16) for z in range(4)]


def scatter_line(sums):
    return [swap(sums[z], "tok", 2 * z) for z in (2, 1, 3)]


def scatter_last(sums, line):
    both = [add_up(sums[0][h], *[p[h] for p in line]) for h in range(2)]
    return both[0] + swap(both[1].astype(BF16), "tok", 8).astype(F32)


def after(value, *gates):
    nothing = add_up(*[g[(0,) * g.ndim] for g in gates]) * 0.0
    return value + nothing.astype(value.dtype)


def dot_nn(a, b):
    return lax.dot_general(a, b, (((1,), (0,)), ((), ())), preferred_element_type=F32)


def dot_nt(a, b):
    return lax.dot_general(a, b, (((1,), (1,)), ((), ())), preferred_element_type=F32)


def dot_tn(a, b):
    return lax.dot_general(a, b, (((0,), (0,)), ((), ())), preferred_element_type=F32)


class Copies:
    def __init__(self, sems):
        self.sems, self.count, self.open = sems, 0, {}

    def start(self, name, *pairs):
        for src, dst in pairs:
            copy = pltpu.make_async_copy(src, dst, self.sems.at[self.count])
            self.count += 1
            copy.start()
            self.open.setdefault(name, []).append(copy)

    def wait(self, *names):
        for name in names:
            for copy in self.open.pop(name):
                copy.wait()

    def finish(self):
        self.wait(*list(self.open))


def over_rows(rows, size, body):
    count = rows // size

    def step(i, carry):
        body(pl.multiple_of(i * size, size), size)
        return carry

    lax.fori_loop(0, count, step, 0)
    if rows % size:
        body(count * size, rows % size)


def over_chunks(rows, count, body):
    step = rows // count // 16 * 16

    def one(i, carry):
        body(pl.multiple_of(i * step, step), step)
        return carry

    lax.fori_loop(0, count - 1, one, 0)
    body((count - 1) * step, rows - (count - 1) * step)


def place(me, slot):
    return pl.ds(pl.multiple_of((me ^ slot) * LANES, LANES), LANES)


def norm_rows(r, blocks, base, row):
    me = r.me[0]
    rows = r.n.shape[0]
    count = len(blocks)
    width = count * LANES

    def body(start, size):
        at = pl.ds(start, size)
        vals = []
        for k, ref in enumerate(blocks):
            v = ref[at, :].astype(F32)
            if base is not None:
                v = v + base[at, place(me, k)]
            r.x[at, place(me, k)] = v
            vals.append(v)
        mean = jnp.sum(functools.reduce(jnp.add, vals), axis=1, keepdims=True) / width
        vals = [v - mean for v in vals]
        spread = functools.reduce(jnp.add, [v * v for v in vals])
        spread = jnp.sum(spread, axis=1, keepdims=True) / width
        scale = lax.rsqrt(spread + EPSILON)
        r.scale[at, :] = jnp.broadcast_to(scale, (size, LANES))
        for k, v in enumerate(vals):
            xh = v * scale
            gain = r.pars[me ^ k, row : row + 1, :]
            shift = r.pars[me ^ k, row + 4 : row + 5, :]
            r.xh[at, place(me, k)] = xh.astype(BF16)
            r.n[at, place(me, k)] = (xh * gain + shift).astype(BF16)

    over_rows(rows, 32, body)


def norm_back_rows(r, blocks):
    me = r.me[0]
    rows = r.low.shape[0]
    width = len(blocks) * LANES

    def body(start, size):
        at = pl.ds(start, size)
        vals = [ref[at, :].astype(F32) for ref in blocks]
        xhs = [r.xh[at, place(me, k)].astype(F32) for k in range(len(blocks))]
        one = jnp.sum(functools.reduce(jnp.add, vals), axis=1, keepdims=True) / width
        two = functools.reduce(jnp.add, [v * x for v, x in zip(vals, xhs)])
        two = jnp.sum(two, axis=1, keepdims=True) / width
        scale = r.scale[at, :]
        for k, (v, x) in enumerate(zip(vals, xhs)):
            g = r.base[at, place(me, k)] + scale * (v - one - x * two)
            r.g[at, place(me, k)] = g
            r.low[at, place(me, k)] = g.astype(BF16)

    over_rows(rows, 32, body)


def partial_blocks(r, left, cols, visit=None):
    parts = [r.p0, r.p1, r.p23.at[0], r.p23.at[1], r.p4, r.p5, r.p67.at[0], r.p67.at[1]]
    me = r.me[0]
    odd = lax.rem(me, 2) == 1
    for k in (2, 6, 4, 0):
        pair = (me // 2) ^ (k // 2)
        start = pl.multiple_of(pair * 2 * LANES, 2 * LANES)
        both = dot_nt(left, r.w[pl.ds(start, 2 * LANES), cols])
        low, high = both[:, :LANES], both[:, LANES:]
        if visit:
            visit(2 * pair, low)
            visit(2 * pair + 1, high)
        low, high = low.astype(BF16), high.astype(BF16)
        parts[k][...] = jnp.where(odd, high, low)
        parts[k + 1][...] = jnp.where(odd, low, high)


def head_mask(h):
    lane = lax.broadcasted_iota(jnp.int32, (1, LANES), 1)
    return (lane >= h * HEAD) & (lane < (h + 1) * HEAD)


def head_scores(query, keys, allowed):
    query = query * jnp.asarray(HEAD ** (-0.5), query.dtype)
    return jnp.where(allowed, dot_nt(query, keys), -1e30)


def only(mask, value):
    return jnp.where(mask, value, jnp.zeros_like(value))


def planes_in(r):
    met = r.met[0]
    shard = r.own.shape[2]
    pairs = []
    for c, plane in enumerate((r.own, r.other)):
        for z in range(4):
            for h in range(2):
                at = (met ^ (8 * h + 2 * z + c)) * shard
                pairs.append((plane.at[z, h], r.w.at[pl.ds(pl.multiple_of(at, shard), shard), :]))
    return pairs


def listed(r, name):
    return [getattr(r, name + str(k)) for k in range(8)]


def attend_kernel(first, row, cut, r):
    copies = Copies(r.sems)
    copies.start("w", *(planes_in(r) if first else [(r.wh.at[:, cut], r.w)]))
    rows = r.n.shape[0]
    blocks = listed(r, "b")
    if first:
        count = r.pars.shape[1]
        for k, ref in enumerate(blocks):
            tail = ref[rows:, :].astype(F32)
            r.pars[r.me[0] ^ k] = tail[:count] + tail[count:]
    norm_rows(r, blocks, None if first else r.base, row)
    copies.start("out", (r.n, r.n_out), (r.xh, r.xh_out), (r.scale, r.scale_out))
    copies.start("out", (r.x, r.x_out))
    copies.wait("w")
    qkv = dot_nn(r.n[...], r.w[:, : 3 * LANES])
    r.qkv[:, :LANES] = (qkv[:, :LANES] + r.qvb[0:1, :]).astype(BF16)
    r.qkv[:, LANES : 2 * LANES] = qkv[:, LANES : 2 * LANES].astype(BF16)
    r.qkv[:, 2 * LANES :] = (qkv[:, 2 * LANES :] + r.qvb[1:2, :]).astype(BF16)
    copies.start("out", (r.qkv, r.qkv_out))
    for h in range(LANES // HEAD):
        values = r.qkv[:, 2 * LANES :]
        r.vh[h] = jnp.where(head_mask(h), values, jnp.ones_like(values))

    def body(start, size):
        at = pl.ds(start, size)
        query = r.qkv[at, :LANES]
        keys = r.qkv[:, LANES : 2 * LANES]
        allowed = r.idc[at, :1] == r.idr[...]
        mixed = jnp.zeros((size, LANES), F32)
        logsum = jnp.zeros((size, LANES), F32)
        for h in range(LANES // HEAD):
            mask = head_mask(h)
            scores = head_scores(only(mask, query), keys, allowed)
            top = jnp.max(scores, axis=1, keepdims=True)
            expo = jnp.exp(scores - top).astype(BF16)
            both = dot_nn(expo, r.vh[h])
            lane = (1 - h) * HEAD
            total = both[:, lane : lane + 1]
            mixed = jnp.where(mask, both * (1.0 / total), mixed)
            logsum = jnp.where(mask, top + jnp.log(total), logsum)
        r.lse[at, :] = logsum
        r.o[at, :] = mixed.astype(BF16)

    over_chunks(rows, 4, body)
    copies.start("out", (r.lse, r.lse_out), (r.o, r.o_out))
    partial_blocks(r, r.o[...], slice(3 * LANES, 4 * LANES))
    copies.finish()


def feed_kernel(row, cut, r):
    copies = Copies(r.sems)
    copies.start("w", (r.wh.at[:, cut], r.w))
    rows, ff = r.h.shape
    norm_rows(r, listed(r, "b"), r.base, row)
    copies.start("out", (r.n, r.n_out), (r.xh, r.xh_out), (r.scale, r.scale_out))
    copies.start("out", (r.x, r.x_out))
    copies.wait("w")
    r.slope[...] = dot_nn(r.n[...], r.w[:, :ff])

    def body(start, size):
        at = pl.ds(start, size)
        u = r.slope[at, :] + r.bias[...]
        phi = 0.5 * (1.0 + lax.erf(u * 0.7071067811865476))
        r.h[at, :] = (u * phi).astype(BF16)
        r.slope[at, :] = phi + u * jnp.exp(-0.5 * u * u) * 0.3989422804014327

    over_rows(rows, 32, body)
    copies.start("out", (r.h, r.h_out), (r.slope, r.slope_out))
    partial_blocks(r, r.h[...], slice(ff, 2 * ff))
    copies.finish()


def feed_back_kernel(first, cut, r):
    copies = Copies(r.sems)
    if not first:
        copies.start("norm", (r.xh_in, r.xh), (r.scale_in, r.scale))
    copies.start("w", (r.wh.at[:, cut], r.w))
    copies.start("slope", (r.slope_in, r.slope))
    me = r.me[0]
    rows, ff = r.slope.shape
    blocks = listed(r, "b")
    if first:

        def copy(start, size):
            at = pl.ds(start, size)
            for k, ref in enumerate(blocks):
                r.low[at, place(me, k)] = ref[at, :]
                r.g[at, place(me, k)] = ref[at, :].astype(F32)

        over_rows(rows, 32, copy)
    else:
        copies.wait("norm")
        norm_back_rows(r, blocks)
    copies.start("out", (r.low, r.low_out), (r.g, r.g_out))
    copies.wait("w")
    r.dh[...] = dot_nn(r.low[...], r.w[:, ff:])
    copies.wait("slope")

    def body(start, size):
        at = pl.ds(start, size)
        r.du[at, :] = (r.dh[at, :] * r.slope[at, :]).astype(BF16)

    over_rows(rows, 32, body)
    copies.start("out", (r.du, r.du_out))
    partial_blocks(r, r.du[...], slice(0, ff))
    copies.finish()


def attend_back_kernel(first, last, cut, r):
    copies = Copies(r.sems)
    copies.start("norm", (r.xh_in, r.xh), (r.scale_in, r.scale))
    copies.start("w", *(planes_in(r) if first else [(r.wh.at[:, cut], r.w)]))
    copies.start("saved", (r.qkv_in, r.qkv), (r.lse_in, r.lse), (r.o_in, r.o))
    rows = r.low.shape[0]
    copies.wait("norm")
    norm_back_rows(r, listed(r, "b"))
    copies.start("out", (r.low, r.low_out), (r.g, r.g_out))
    if last:
        copies.start("up", (r.xu_in, r.xh))
    copies.wait("w", "saved")
    r.do[...] = dot_nn(r.low[...], r.w[:, 3 * LANES :]).astype(BF16)
    scale = HEAD ** (-0.5)

    def head(h, carry):
        mask = head_mask(h)

        def body(start, size):
            at = pl.ds(start, size)
            keys = r.qkv[:, LANES : 2 * LANES]
            allowed = r.idc[at, :1] == r.idr[...]
            scores = head_scores(only(mask, r.qkv[at, :LANES]), keys, allowed)
            logsum = jnp.max(jnp.where(mask, r.lse[at, :], -3e38), axis=1, keepdims=True)
            probs = jnp.exp(scores - logsum)
            r.probs[at, :] = probs.astype(BF16)
            dmix = only(mask, r.do[at, :])
            dprobs = dot_nt(dmix, r.qkv[:, 2 * LANES :])
            centre = dmix.astype(F32) * r.o[at, :].astype(F32)
            centre = jnp.sum(centre, axis=1, keepdims=True)
            ds = (probs * (dprobs - centre)).astype(BF16)
            r.ds[at, :] = ds
            dq = (dot_nn(ds, keys) * scale).astype(BF16)
            r.dproj[at, :LANES] = jnp.where(mask, dq, r.dproj[at, :LANES])

        over_chunks(rows, 4, body)
        at = slice(LANES, 2 * LANES)
        dk = (dot_tn(r.ds[...], r.qkv[:, :LANES]) * scale).astype(BF16)
        r.dproj[:, at] = jnp.where(mask, dk, r.dproj[:, at])
        at = slice(2 * LANES, 3 * LANES)
        dv = dot_tn(r.probs[...], r.do[...]).astype(BF16)
        r.dproj[:, at] = jnp.where(mask, dv, r.dproj[:, at])
        return carry

    lax.fori_loop(0, LANES // HEAD, head, 0)
    copies.start("out", (r.dproj, r.dproj_out))
    visit = None
    if last:
        copies.wait("up")
        sums = [jnp.zeros((rows, LANES), F32), jnp.zeros((rows, LANES), F32)]

        def visit(j, part):
            gain = r.pars[j, 0:1, :]
            lanes = pl.ds(pl.multiple_of(j * LANES, LANES), LANES)
            both = part * r.xh[:, lanes].astype(F32)
            sums[0] = sums[0] + part * gain
            sums[1] = sums[1] + both * gain
            r.cols[j, 0:1, :] = jnp.sum(both, axis=0, keepdims=True)
            r.cols[j, 1:2, :] = jnp.sum(part, axis=0, keepdims=True)

    partial_blocks(r, r.dproj[...], slice(0, 3 * LANES), visit)
    if last:
        one, two = [jnp.sum(v, axis=1, keepdims=True) for v in sums]
        r.sums[...] = jnp.where(head_mask(0), one, two)
    copies.finish()


def weight_grad_kernel(terms, r):
    copies = Copies(r.sems)
    for t in range(terms):
        for name in ("x", "y"):
            name += str(t)
            copies.start(t, (getattr(r, name + "_in"), getattr(r, name)))
    width = r.x0.shape[1]
    step, shard = 256, width // 16
    met = r.met[0]
    own = pl.ds(pl.multiple_of(r.me[0] * LANES, LANES), LANES)
    ones = jnp.ones((8, r.x0.shape[0]), BF16)
    at = 0
    for t in range(terms):
        copies.wait(t)
        x, y = getattr(r, "x" + str(t)), getattr(r, "y" + str(t))
        cols = slice(at, at + y.shape[1])
        at += y.shape[1]
        for i in range(0, width, step):
            d = dot_tn(x[:, i : i + step], y[...]).astype(BF16)
            if len(r.out.shape) == 2:
                r.out[i : i + step, cols] = d
                continue
            for s in range(0, step, shard):
                to = met ^ ((i + s) // shard)
                c, z, h = to & 1, (to >> 1) & 3, to >> 3
                r.out[c, z, h, :, cols] = d[s : s + shard]
        if t % 2 == 0:
            getattr(r, "ysum" + str(t))[...] = dot_nn(ones, y[...])
        else:
            getattr(r, "xsum" + str(t))[...] = dot_nn(ones, x[:, own])
    if hasattr(r, "out_hbm"):
        copies.start("out", (r.out, r.out_hbm))
    copies.finish()


class Far:
    def __init__(self, value):
        self.value = value


def whole(name, kernel, ins, outs, scratch, flops, sems):
    vmem = pl.BlockSpec(memory_space=pltpu.VMEM)
    smem = pl.BlockSpec(memory_space=pltpu.SMEM)
    far = pl.BlockSpec(memory_space=pltpu.HBM)

    def spec(v):
        return far if isinstance(v, Far) else smem if v.shape == (1,) else vmem

    def plain(v):
        return v.value if isinstance(v, Far) else v

    names = [*ins, *outs, *scratch, "sems"]

    def body(*refs):
        kernel(types.SimpleNamespace(**dict(zip(names, refs))))

    def pinned(v):
        if isinstance(v, Far):
            return pltpu.with_memory_space_constraint(v.value, pltpu.HBM)
        return v

    def shaped(v):
        return pltpu.HBM(v.value.shape, v.value.dtype) if isinstance(v, Far) else v

    args = [plain(v) for v in ins.values()]
    shapes = [plain(v) for v in outs.values()]
    size = sum(a.size * a.dtype.itemsize for a in [*args, *shapes])
    results = pl.pallas_call(
        body,
        out_shape=[shaped(v) for v in outs.values()],
        in_specs=[spec(v) for v in ins.values()],
        out_specs=[spec(v) for v in outs.values()],
        scratch_shapes=[pltpu.VMEM(v.shape, v.dtype) for v in scratch.values()]
        + [pltpu.SemaphoreType.DMA((sems,))],
        compiler_params=pltpu.CompilerParams(vmem_limit_bytes=VMEM_LIMIT),
        cost_estimate=pl.CostEstimate(flops=flops, bytes_accessed=size, transcendentals=0),
        name=name,
    )(*[pinned(v) for v in ins.values()])
    return types.SimpleNamespace(**dict(zip(outs, results)))


def numbered(name, values):
    return {name + str(k): v for k, v in enumerate(values)}


def shards(
    tokens,
    image_ids,
    norm_gains,
    norm_shifts,
    qkv_weight,
    qv_bias,
    out_weight,
    out_bias,
    up_weight,
    up_bias,
    down_weight,
    down_bias,
    out_grad,
):
    rows, cols = tokens.shape
    peers = lax.axis_size("wid")
    width = cols * peers
    ff = up_weight.shape[2]
    mix = 4 * cols
    me = lax.axis_index("wid")
    here = {
        "me": me.astype(jnp.int32).reshape(1),
        "met": lax.axis_index("tok").astype(jnp.int32).reshape(1),
    }
    shard = width // lax.axis_size("tok")

    def arr(dtype, *shape):
        return jax.ShapeDtypeStruct(shape, dtype)

    full32, full16 = arr(F32, rows, width), arr(BF16, rows, width)
    own32, own16 = arr(F32, rows, cols), arr(BF16, rows, cols)
    ff32, ff16 = arr(F32, rows, ff), arr(BF16, rows, ff)
    qkv16 = arr(BF16, rows, 3 * cols)
    pair16 = arr(BF16, 2, rows, cols)
    parts = {"p0": own16, "p1": own16, "p23": pair16, "p4": own16, "p5": own16, "p67": pair16}

    def listed_parts(result):
        return [getattr(result, name) for name in parts]

    down_t = jnp.swapaxes(down_weight, 1, 2)
    out_t = jnp.swapaxes(out_weight, 1, 2)
    mix_local = [
        jnp.concatenate([qkv_weight[l].reshape(-1, 3 * cols), out_t[l]], axis=1)
        for l in range(LAYERS)
    ]
    feed_local = [jnp.concatenate([up_weight[l], down_t[l]], axis=1) for l in range(LAYERS)]

    small = jnp.concatenate([norm_gains.reshape(-1, cols), norm_shifts.reshape(-1, cols)])
    high = lax.reduce_precision(small, 8, 7)
    rest = lax.reduce_precision(small - high, 8, 7)
    blocks = gather_blocks(
        jnp.concatenate([tokens, high.astype(BF16), rest.astype(BF16)], axis=0)
    )
    own_plane, other_plane = gather_planes(
        mix_local[0], [blocks[k] for k in (1, 2, 4, 6)], [blocks[k] for k in (3, 5, 7)]
    )
    feed0 = lax.all_gather(feed_local[0], "tok", axis=0, tiled=True)
    both1 = lax.all_gather(
        jnp.concatenate([mix_local[1], feed_local[1]], axis=1), "tok", axis=0, tiled=True
    )
    mix_w = [{"own": Far(own_plane), "other": Far(other_plane)}, {"wh": Far(both1)}]
    feed_w = [{"wh": Far(feed0)}, {"wh": Far(both1)}]
    mix_cut = slice(0, mix)
    feed_cut = [slice(0, 2 * ff), slice(mix, mix + 2 * ff)]

    ids = {
        "idr": image_ids.reshape(1, rows),
        "idc": jnp.broadcast_to(image_ids[:, None], (rows, LANES)),
    }
    w_mix, w_feed = {"w": arr(BF16, width, mix)}, {"w": arr(BF16, width, 2 * ff)}
    norm_out = {"n_out": Far(full16), "xh_out": Far(full16), "scale_out": Far(own32)}
    norm_scratch = {"n": full16, "xh": full16, "scale": own32, "x": full32}
    pars_shape = arr(F32, peers, *small.shape)

    mm = 2 * rows * width
    base = pars = None
    saved = []
    for l in range(LAYERS):
        first = base is None
        a = whole(
            "attend",
            functools.partial(attend_kernel, first, 2 * l, mix_cut),
            {
                **here,
                **ids,
                **mix_w[l],
                **numbered("b", blocks),
                "qvb": qv_bias[l],
                **({} if first else {"base": base, "pars": pars}),
            },
            {
                "x_out": Far(full32),
                **norm_out,
                "qkv_out": Far(qkv16),
                "lse_out": Far(own32),
                "o_out": Far(own16),
                **parts,
                **({"pars": pars_shape} if first else {}),
            },
            {**norm_scratch, **w_mix, "qkv": qkv16, "lse": own32, "o": own16, "vh": pair16},
            mm * mix + 8 * rows * rows * cols,
            36,
        )
        if first:
            pars = a.pars
        blocks = gather_blocks((reduce_blocks(listed_parts(a))[0] + out_bias[l]).astype(BF16))
        f = whole(
            "feed",
            functools.partial(feed_kernel, 2 * l + 1, feed_cut[l]),
            {
                **here,
                **feed_w[l],
                **numbered("b", blocks),
                "bias": up_bias[l].reshape(1, ff),
                "base": a.x_out,
                "pars": pars,
            },
            {"x_out": Far(full32), **norm_out, "h_out": Far(ff16), "slope_out": Far(ff32), **parts},
            {**norm_scratch, **w_feed, "h": ff16, "slope": ff32},
            mm * 2 * ff,
            20,
        )
        branch = reduce_blocks(listed_parts(f))[0] + down_bias[l]
        base = f.x_out
        if l + 1 < LAYERS:
            blocks = gather_blocks(branch.astype(BF16))
            grad_blocks = gather_blocks(after(out_grad, blocks[7]))
        saved.append((a, f))

    def own(value):
        return lax.dynamic_slice_in_dim(value, me * cols, cols, 1).astype(F32)

    activations = (own(base) + branch).astype(BF16)

    blocks = grad_blocks
    g = up = None
    back_scratch = {"low": full16, "xh": full16, "scale": own32, "g": full32}
    lines, scattered = [], []
    for l in reversed(range(LAYERS)):
        a, f = saved[l]
        top, last = g is None, l == 0
        b = whole(
            "feed_back",
            functools.partial(feed_back_kernel, top, feed_cut[l]),
            {
                **here,
                **feed_w[l],
                **numbered("b", blocks),
                "slope_in": Far(f.slope_out),
                **({} if top else {"base": g, **up}),
            },
            {"g_out": Far(full32), "low_out": Far(full16), "du_out": Far(ff16), **parts},
            {**back_scratch, **w_feed, "slope": ff32, "dh": ff32, "du": ff16},
            mm * 2 * ff,
            20,
        )
        g = b.g_out

        def grads(name, gate, *pairs):
            total = sum(y.shape[1] for _, y in pairs)
            shape = arr(BF16, 2, 4, 2, shard, total) if last else arr(BF16, width, total)
            ins, outs, scratch = dict(here), {}, {}
            if gate is not None:
                ins["met"] = after(ins["met"], gate)
            for t, pair in enumerate(pairs):
                for n, v in zip(("x", "y"), pair):
                    ins[n + str(t) + "_in"] = Far(v)
                    scratch[n + str(t)] = arr(BF16, *v.shape)
                if t % 2:
                    outs["xsum" + str(t)] = arr(F32, 8, LANES)
                else:
                    outs["ysum" + str(t)] = arr(F32, 8, pair[1].shape[1])
            outs |= {"out": shape} if last else {"out_hbm": Far(shape)}
            if not last:
                scratch["out"] = shape
            kernel = functools.partial(weight_grad_kernel, len(pairs))
            return whole(name, kernel, ins, outs, scratch, mm * total, 10)

        dn2, sign = reduce_blocks(listed_parts(b))
        blocks = gather_blocks((dn2 * norm_gains[l, 1]).astype(BF16))
        feed_pairs = ((f.n_out, b.du_out), (b.low_out, f.h_out))
        if last:
            fg = grads("feed_grad", sign, *feed_pairs)
            blocks, feed_sums = lax.optimization_barrier((blocks, scatter_pairs(fg.out)))
            feed_line = scatter_line(feed_sums)
        c = whole(
            "attend_back",
            functools.partial(attend_back_kernel, l == 0, last, mix_cut),
            {
                **here,
                **ids,
                **mix_w[l],
                **numbered("b", blocks),
                "base": g,
                "xh_in": Far(f.xh_out),
                "scale_in": Far(f.scale_out),
                "qkv_in": Far(a.qkv_out),
                "lse_in": Far(a.lse_out),
                "o_in": Far(a.o_out),
                **({"xu_in": Far(a.xh_out), "pars": pars} if last else {}),
            },
            {
                "g_out": Far(full32),
                "low_out": Far(full16),
                "dproj_out": Far(qkv16),
                **parts,
                **({"sums": own32, "cols": arr(F32, peers, 8, cols)} if last else {}),
            },
            {
                **back_scratch,
                **w_mix,
                "qkv": qkv16,
                "lse": own32,
                "dproj": qkv16,
                "do": own16,
                "o": own16,
                "probs": arr(BF16, rows, rows),
                "ds": arr(BF16, rows, rows),
            },
            mm * mix + 20 * rows * rows * cols,
            36,
        )
        g = c.g_out
        dn1, sign = reduce_blocks(listed_parts(c))
        mix_pairs = ((a.n_out, c.dproj_out), (c.low_out, a.o_out))
        if last:
            ag = grads("attend_grad", None, *mix_pairs)
            mix_cols, feed_cols = (ag.ysum0, ag.xsum1), (fg.ysum0, fg.xsum1)
        else:
            ag = grads("layer_grad", sign, *mix_pairs, *feed_pairs)
            mix_cols, feed_cols = (ag.ysum0, ag.xsum1), (ag.ysum2, ag.xsum3)
        if last:
            mix_sums = scatter_pairs(ag.out)
            sums = after(c.sums, mix_sums[0])
            message = jnp.concatenate([sums[:, 0], sums[:, HEAD]])
            message = jnp.broadcast_to(message, (peers, 2 * rows))
            message = jnp.concatenate([message, c.cols[:, :2].reshape(peers, -1)], axis=1)
            message = lax.all_to_all(message, "wid", 0, 0, tiled=True).sum(axis=0)
        own1, own2 = own(a.xh_out), own(f.xh_out)
        a1 = dn1 * norm_gains[l, 0]
        if last:
            one, two = message[:rows, None] / width, message[rows : 2 * rows, None] / width
            input_grad = own(g) + a.scale_out * (a1 - one - own1 * two)
            first_norm = list(message[2 * rows :].reshape(2, cols))
            feed_part = scatter_last(feed_sums, feed_line)
            scattered.append([feed_part, scatter_last(mix_sums, scatter_line(mix_sums))])
        else:
            blocks = gather_blocks(a1.astype(BF16))
            up = {"xh_in": Far(a.xh_out), "scale_in": Far(a.scale_out)}
            first_norm = [jnp.sum(dn1 * own1, axis=0), jnp.sum(dn1, axis=0)]
            both = lax.psum_scatter(ag.out_hbm, "tok", scatter_dimension=0, tiled=True)
            both = both.astype(F32)
            scattered.append([both[:, mix:], both[:, :mix]])
        vectors = [
            first_norm[0],
            jnp.sum(dn2 * own2, axis=0),
            first_norm[1],
            jnp.sum(dn2, axis=0),
            mix_cols[0][0, :cols],
            mix_cols[0][0, 2 * cols :],
            mix_cols[1][0],
            feed_cols[1][0],
            feed_cols[0][0],
        ]
        lines.append(jnp.concatenate(vectors).reshape(-1, cols))
    lines = copies_to_all(jnp.stack(lines[::-1]), "tok")
    lines = lines.reshape(-1, LAYERS, *lines.shape[1:]) if lines.ndim == 3 else lines
    lines = lines.sum(axis=0)
    scattered = scattered[::-1]

    def stack(pick):
        return jnp.stack([pick(lines[l], scattered[l]) for l in range(LAYERS)])

    return (
        activations,
        input_grad,
        stack(lambda v, b: v[0:2]),
        stack(lambda v, b: v[2:4]),
        stack(lambda v, b: b[1][:, : 3 * cols].reshape(-1, 3, cols)),
        stack(lambda v, b: v[4:6]),
        jnp.swapaxes(stack(lambda v, b: b[1][:, 3 * cols :]), 1, 2),
        stack(lambda v, b: v[6]),
        stack(lambda v, b: b[0][:, :ff]),
        stack(lambda v, b: v[8:].reshape(-1)),
        jnp.swapaxes(stack(lambda v, b: b[0][:, ff:]), 1, 2),
        stack(lambda v, b: v[7]),
    )


def solution(mesh):
    placed = (
        P("tok", "wid"),
        P("tok"),
        P(None, None, "wid"),
        P(None, None, "wid"),
        P(None, "tok", None, "wid"),
        P(None, None, "wid"),
        P(None, "wid", "tok"),
        P(None, "wid"),
        P(None, "tok", "wid"),
        P(None, "wid"),
        P(None, "wid", "tok"),
        P(None, "wid"),
        P("tok", "wid"),
    )
    return jax.shard_map(
        shards,
        mesh=mesh,
        in_specs=placed,
        out_specs=(
            P("tok", "wid"),
            P("tok", "wid"),
            P(None, None, "wid"),
            P(None, None, "wid"),
            P(None, "tok", None, "wid"),
            P(None, None, "wid"),
            P(None, "wid", "tok"),
            P(None, "wid"),
            P(None, "tok", "wid"),
            P(None, "wid"),
            P(None, "wid", "tok"),
            P(None, "wid"),
        ),
        check_vma=False,
    )
```
